512 devices in a mesh: region: 32 (over x, y), shard: 16 (over z, core).
Axes of the slice: x: 4, y: 8, z: 8, core: 2. Of those that a mesh axis runs over, the one named last changes fastest.
Arguments:
- planes: bfloat16 [4, 16384, 512], P(None, ('region', 'shard')), may hold values from -6 to 6
- sed_weights: float32 [6, 4], replicated, may hold values from 0.1 to 2
- psf_taps: float32 [2, 6, 3, 25], replicated, may hold values from 0.004 to 0.08
- resample_rows: bfloat16 [16384, 128, 128], P(('region', 'shard')), may hold values from -0.5 to 0.5
- resample_cols: bfloat16 [16384, 128, 256], P(('region', 'shard')), may hold values from -0.375 to 0.375
- observed: bfloat16 [16384, 128, 128], P(('region', 'shard')), may hold values from -6 to 6
- exposure_meta: int32 [3, 16384], P(None, 'region'), may hold values from 0 to 15, as said below
- slot_counts: int32 [32, 16], P('region'), may hold values from 8 to 32, as said below
Outputs:
- plane_grad: float32 [4, 16384, 512], P(None, ('region', 'shard'))
The draws below stay inside these ranges and needn't reach their ends.
Inputs may be any that keep to these rules, and one draw needn't show every extreme that they name: `exposure_meta`: row 0 is a row tile of the exposure's region, 0 to 15; row 1 a column tile, 0 to 1; row 2 a band, 0 to 5. `slot_counts`: the live slots of a device are its first ones. In every region one device has all 32 slots live, the others between 8 and 16.
All inputs are finite; a program needn't handle non-finite values.
Results may differ from the reference program's by a relative error of at most 0.003.
Values may be sent and summed in bfloat16 or wider, within the bound.
A program may use at most 64 MiB of HBM per device.

```python
import math
import jax
import jax.numpy as jnp
from jax import lax

COMPONENTS = 4
BANDS = 6
TERMS = 3
TAPS = 25
TILE_ROWS = 32
COLS = 512
WIN_Y = 128
WIN_X = 256
OUT = 128
E_SLOT = 32
REGIONS = 32
SHARDS = 16
ROWS = 16384
EXPOSURES = 16384
N_SHARD = 16


def draw_exposure_meta(key, part):
    row_tile = jax.random.randint(jax.random.fold_in(key, 11), (EXPOSURES,), 0, SHARDS)
    col_tile = jax.random.randint(jax.random.fold_in(key, 12), (EXPOSURES,), 0, COLS // WIN_X)
    band = jax.random.randint(jax.random.fold_in(key, 13), (EXPOSURES,), 0, BANDS)
    return jnp.stack([row_tile, col_tile, band]).astype(jnp.int32)


def draw_slot_counts(key, part):
    base = jax.random.randint(jax.random.fold_in(key, 21), (REGIONS, SHARDS), E_SLOT // 4, E_SLOT // 2 + 1)
    full = jax.random.randint(jax.random.fold_in(key, 22), (REGIONS,), 0, SHARDS)
    column = jnp.arange(SHARDS, dtype=jnp.int32)[None, :]
    return jnp.where(column == full[:, None], E_SLOT, base).astype(jnp.int32)


def shard_levels(stream_key, dims, pieces, low, top_value):
    factor_of, own = 1.0, jax.random.fold_in(stream_key, 6)
    for axis_at, shards_of in pieces:
        steps = jnp.exp(jax.random.uniform(jax.random.fold_in(own, axis_at), (shards_of,), jnp.float32, low / len(pieces), top_value / len(pieces)))
        factor_of = factor_of * jnp.repeat(steps, dims[axis_at] // shards_of).reshape([-1 if axis == axis_at else 1 for axis in range(len(dims))])
    return factor_of


def centred(rng, extent, spread, most, cuts=(), kind=jnp.bfloat16):
    result = spread * jax.random.normal(rng, extent, jnp.float32)
    if cuts:
        result = result * shard_levels(rng, extent, cuts, -0.22, 0.18)
    return jnp.clip(result, -most, most).astype(kind)


def setup_inputs(seed: int = 0) -> dict:
    key_list = jax.random.split(jax.random.key(seed), 9)
    return {
        "planes": centred(key_list[0], (COMPONENTS, ROWS, COLS), 1.0, 6.0, ((1, 512),)),
        "sed_weights": jnp.clip(jnp.exp(jax.random.uniform(key_list[1], (BANDS, COMPONENTS), jnp.float32, math.log(0.1), math.log(2.0))), 0.1, 2.0),
        "psf_taps": jnp.clip(jnp.exp(jax.random.uniform(key_list[2], (2, BANDS, TERMS, TAPS), jnp.float32, math.log(0.004), math.log(0.08))), 0.004, 0.08),
        "resample_rows": centred(key_list[3], (EXPOSURES, OUT, WIN_Y), WIN_Y ** -0.5, 0.5, ((0, 512),)),
        "resample_cols": centred(key_list[4], (EXPOSURES, OUT, WIN_X), WIN_X ** -0.5, 0.375, ((0, 512),)),
        "observed": centred(key_list[5], (EXPOSURES, OUT, OUT), 1.0, 6.0, ((0, 512),)),
        "exposure_meta": draw_exposure_meta(jax.random.fold_in(key_list[8], 71), 0),
        "slot_counts": draw_slot_counts(jax.random.fold_in(key_list[8], 71), 0),
    }


def settle(value):
    return lax.optimization_barrier(value.astype(jnp.bfloat16)).astype(jnp.float32)


def band_tables(taps, width):
    tap_count = taps.shape[-1]
    offset = jnp.arange(width, dtype=jnp.int32)[:, None] - jnp.arange(width, dtype=jnp.int32)[None, :] + tap_count // 2
    selector = (offset[None, :, :] == jnp.arange(tap_count, dtype=jnp.int32)[:, None, None]).astype(jnp.float32)
    return jnp.einsum("btk,kij->btij", taps.astype(jnp.float32), selector, precision=lax.Precision.HIGHEST).astype(jnp.bfloat16)


def exposure_gradient(window, sed_row, rows_band, cols_band, row_map, col_map, pixels):
    py_mat = rows_band.astype(jnp.float32)
    px_mat = cols_band.astype(jnp.float32)
    ry_mat = row_map.astype(jnp.float32)
    rx_mat = col_map.astype(jnp.float32)
    mixed = settle(jnp.sum(sed_row[:, None, None] * window, axis=0))
    smeared = settle(jnp.einsum("tiy,yx->tix", py_mat, mixed))
    blurred = settle(jnp.einsum("tix,tjx->ij", smeared, px_mat))
    sampled = settle(jnp.einsum("oy,yx->ox", ry_mat, blurred))
    model = jnp.einsum("ox,px->op", sampled, rx_mat)
    misfit = settle(model - pixels.astype(jnp.float32))
    back_rows = settle(jnp.einsum("oy,op->yp", ry_mat, misfit))
    back = settle(jnp.einsum("yp,px->yx", back_rows, rx_mat))
    unsmeared = settle(jnp.einsum("tiy,ix->tyx", py_mat, back))
    return jnp.einsum("tyj,tjx->yx", unsmeared, px_mat)


def reference(planes, sed_weights, psf_taps, resample_rows, resample_cols, observed, exposure_meta, slot_counts):
    region_rows = TILE_ROWS * N_SHARD
    rim_rows = WIN_Y - TILE_ROWS
    padded = jnp.concatenate([planes, jnp.zeros((COMPONENTS, rim_rows, COLS), planes.dtype)], axis=1)
    rows_tab = band_tables(psf_taps[0], WIN_Y)
    cols_tab = band_tables(psf_taps[1], WIN_X)
    per_region = N_SHARD * E_SLOT

    def visit(gradient, slot):
        region = slot // per_region
        device = (slot % per_region) // E_SLOT
        local = slot % E_SLOT
        count = slot_counts[region, device]

        def work(current):
            row_start = (region * region_rows + exposure_meta[0, slot] * TILE_ROWS).astype(jnp.int32)
            col_start = (exposure_meta[1, slot] * WIN_X).astype(jnp.int32)
            band = exposure_meta[2, slot]
            zero = jnp.zeros((), jnp.int32)
            window = lax.dynamic_slice(padded, (zero, row_start, col_start), (COMPONENTS, WIN_Y, WIN_X)).astype(jnp.float32)
            sed_row = sed_weights[band]
            window_grad = exposure_gradient(window, sed_row, rows_tab[band], cols_tab[band], resample_rows[slot], resample_cols[slot], observed[slot])
            part = lax.dynamic_slice(current, (zero, row_start, col_start), (COMPONENTS, WIN_Y, WIN_X))
            return lax.dynamic_update_slice(current, part + sed_row[:, None, None] * window_grad[None], (zero, row_start, col_start))

        return lax.cond(local < count, work, lambda current: current, gradient), None

    start = jnp.zeros((COMPONENTS, ROWS + rim_rows, COLS), jnp.float32)
    gradient, _ = lax.scan(visit, start, jnp.arange(EXPOSURES, dtype=jnp.int32))
    return gradient[:, :ROWS]
```

```python
import functools

import jax
import jax.numpy as jnp
from jax import lax
from jax.experimental import pallas as pl
from jax.experimental.pallas import tpu as pltpu
from jax.sharding import PartitionSpec as P

F32 = jnp.float32
BF16 = jnp.bfloat16
GROUP = 4


def passed_along(block, axis, distance):
    devices = range(lax.axis_size(axis))
    route = [(i - distance, i) for i in devices if i - distance in devices]
    return lax.ppermute(block, axis, route)


def dot(a, b, ca=1, cb=0):
    return lax.dot_general(a, b, (((ca,), (cb,)), ((), ())), preferred_element_type=F32)


def toeplitz(base, size):
    wide = jnp.broadcast_to(base, (size, base.shape[-1]))
    return pltpu.roll(wide, 0, 1, stride=1, stride_axis=0)[:, :size].astype(BF16)


def bases(taps, size):
    count = taps.shape[-1]
    half, length = count // 2, size + 128
    flat = taps.reshape(-1, 1, count)

    def place(v):
        gap = jnp.zeros(v.shape[:-1] + (length - count,), F32)
        return jnp.concatenate([v[..., half:], gap, v[..., :half]], axis=-1)

    return jnp.stack([place(flat[..., ::-1]), place(flat)], axis=1).reshape(-1, 1, length)


def grad_kernel(
    bands, terms, tile,
    counts, meta, sed, rbase, cbase, planes, ry_hbm, rx_hbm, ob_hbm,
    out,
    ry, rx, ob, rows_tab, rows_tab_t, cols_tab, cols_tab_t, sems,
):
    me = lax.axis_index("shard")
    slots, _, wy = ry.shape
    wx = rx.shape[2]
    comps = planes.shape[0]
    count = counts[0, me]
    turns = (count + GROUP - 1) // GROUP
    pairs = ((ry_hbm, ry), (rx_hbm, rx), (ob_hbm, ob))

    def copies(turn):
        part = pl.ds(turn * GROUP, GROUP)
        return [
            pltpu.make_async_copy(far.at[part], near.at[part], sems.at[j, turn])
            for j, (far, near) in enumerate(pairs)
        ]

    @pl.loop(0, turns)
    def _(turn):
        for copy in copies(turn):
            copy.start()

    @pl.loop(0, bands)
    def _(band):
        for t in range(terms):
            for d in range(2):
                at = (band * terms + t) * 2 + d
                (rows_tab, rows_tab_t)[d][band, :, t * wy : (t + 1) * wy] = toeplitz(rbase[at], wy)
                (cols_tab, cols_tab_t)[d][band, :, t * wx : (t + 1) * wx] = toeplitz(cbase[at], wx)

    out[...] = jnp.zeros_like(out)

    def stack(a, width):
        return jnp.concatenate([a[:, t * width : (t + 1) * width] for t in range(terms)], axis=0)

    @pl.loop(0, turns)
    def _(turn):
        for copy in copies(turn):
            copy.wait()
        members = range(GROUP)
        slot = [turn * GROUP + g for g in members]
        at = [me * slots + e for e in slot]
        band = [meta[2, p] for p in at]
        window = [
            (
                pl.ds(pl.multiple_of(meta[0, p] * tile, tile), wy),
                pl.ds(pl.multiple_of(meta[1, p] * wx, wx), wx),
            )
            for p in at
        ]
        mixed = [
            sum(sed[band[g], k] * planes[(k,) + window[g]].astype(F32) for k in range(comps)).astype(BF16)
            for g in members
        ]
        smeared = [dot(mixed[g], cols_tab_t[band[g]]).astype(BF16) for g in members]
        blurred = [dot(rows_tab[band[g]], stack(smeared[g], wx)).astype(BF16) for g in members]
        sampled = [dot(ry[slot[g]], blurred[g]).astype(BF16) for g in members]
        misfit = [
            (dot(sampled[g], rx[slot[g]], 1, 1) - ob[slot[g]].astype(F32)).astype(BF16) for g in members
        ]
        back_rows = [dot(ry[slot[g]], misfit[g], 0, 0).astype(BF16) for g in members]
        back = [dot(back_rows[g], rx[slot[g]]).astype(BF16) for g in members]
        unsmeared = [dot(back[g], cols_tab[band[g]]).astype(BF16) for g in members]
        window_grad = [dot(rows_tab_t[band[g]], stack(unsmeared[g], wx)) for g in members]
        for g in members:
            usable = slot[g] < count
            for k in range(comps):
                weight = jnp.where(usable, sed[band[g], k], 0.0)
                part = (k,) + window[g]
                out[part] = out[part] + weight * window_grad[g]


def gradient_of(planes, sed, taps, ry, rx, ob, meta, counts, tile):
    slots, _, wy = ry.shape
    wx = rx.shape[2]
    bands, terms = taps.shape[1:3]
    scalars = pl.BlockSpec(memory_space=pltpu.SMEM)
    near = pl.BlockSpec(memory_space=pltpu.VMEM)
    far = pl.BlockSpec(memory_space=pl.ANY)
    tables = [(bands, wy, terms * wy)] * 2 + [(bands, wx, terms * wx)] * 2
    return pl.pallas_call(
        functools.partial(grad_kernel, bands, terms, tile),
        out_shape=jax.ShapeDtypeStruct(planes.shape, F32),
        in_specs=[scalars] * 3 + [near] * 3 + [far] * 3,
        out_specs=near,
        scratch_shapes=[pltpu.VMEM(a.shape, a.dtype) for a in (ry, rx, ob)]
        + [pltpu.VMEM(shape, BF16) for shape in tables]
        + [pltpu.SemaphoreType.DMA((3, slots // GROUP))],
        compiler_params=pltpu.CompilerParams(vmem_limit_bytes=56 << 20),
    )(counts, meta, sed, bases(taps[0], wy), bases(taps[1], wx), planes, ry, rx, ob)


def local(planes, sed, taps, ry, rx, ob, meta, counts):
    tile = planes.shape[1]
    region_rows = tile * lax.axis_size("shard")
    rim_rows = ry.shape[2] - tile
    gathered = lax.all_gather(planes, "shard", axis=1, tiled=True)
    next_part = passed_along(gathered[:, :rim_rows], "region", -1)
    extended = jnp.concatenate([gathered, next_part], axis=1)
    gradient = gradient_of(extended, sed, taps, ry, rx, ob, meta, counts, tile)
    incoming = passed_along(gradient[:, region_rows:], "region", 1)
    own_rows = gradient[:, :region_rows].at[:, :rim_rows].add(incoming)
    return lax.psum_scatter(own_rows, "shard", scatter_dimension=1, tiled=True)


def solution(mesh):
    shards = P(("region", "shard"), None, None)
    placed = (P(None, ("region", "shard"), None), P(), P(), shards, shards, shards)
    placed += (P(None, "region"), P("region", None))
    return jax.shard_map(
        local,
        mesh=mesh,
        in_specs=placed,
        out_specs=P(None, ("region", "shard"), None),
        check_vma=False,
    )
```
